32 devices in a mesh: lat: 4 (over y, x), lon: 8 (over z, core).
Axes of the slice: x: 2, y: 2, z: 4, core: 2. Of those that a mesh axis runs over, the one named last changes fastest.
Arguments:
- fields: bfloat16 [16, 720, 641], P('lat', 'lon'), may hold values from -36 to 36
- group_size: int32 [8], replicated, may hold values from 1 to 121, 641 in all
- band_of_row: int32 [16], P('lat'), may hold values from 0 to 7, never falling along the last dimension, each value on 1 to 4 neighbouring positions
- basis_spectra: float32 [8, 9, 8, 2, 361], replicated, may hold values from -0.75 to 0.75
- basis_coef: float32 [641, 8], replicated, may hold values from -5 to 5
- mlp_gain: float32 [641], replicated, may hold values from 0.25 to 1.75
- w_in: bfloat16 [641, 1282], replicated, may hold values from -0.25 to 0.25
- w_out: bfloat16 [1282, 641], replicated, may hold values from -0.15625 to 0.15625
Outputs:
- block_out: bfloat16 [16, 720, 641], P('lat', 'lon')
The draws below stay inside these ranges and needn't reach their ends.
Inputs may be any that keep to these rules, and one draw needn't show every extreme that they name: `group_size`: group j holds the channels that follow those of groups 0 to j - 1; the sizes sum to 641. `band_of_row`: band numbers never fall along latitude; every band covers 1 to 4 rows.
All inputs are finite; a program needn't handle non-finite values.
Results may differ from the reference program's by a relative error of at most 0.0051.
Values may be sent and summed in bfloat16 or wider, within the bound.
A program may use at most 64 MiB of HBM per device.

```python
import math
import jax
import jax.numpy as jnp
import numpy as np
from jax import lax

C = 641
HIDDEN_UNITS = 1282
NLON = 720
HALO = 4
NBASIS = 8
BANDS = 8
NLAT = 16
GROUPS = 8
GMAX = 121
FREQ = 361
BAND_MOST = 4


def draw_fields(key, part):
    key_base = jax.random.fold_in(key, 11)
    key_chan = jax.random.fold_in(key, 12)
    key_lon = jax.random.fold_in(key, 13)
    chan_scale = jnp.exp(jax.random.uniform(key_chan, (C,), jnp.float32, math.log(0.3), math.log(3.0)))
    lon_scale = jnp.exp(jax.random.uniform(key_lon, (NLON, 1), jnp.float32, math.log(0.3), math.log(3.0)))
    base = jnp.clip(jax.random.normal(key_base, (NLAT, NLON, C), jnp.float32), -4.0, 4.0)
    return (base * lon_scale * chan_scale).astype(jnp.bfloat16)


def length_profile(amount, total, most, lean):
    weights = [(1 << 20) // math.isqrt(grade ** lean) + 1 for grade in range(2, amount + 1)]
    rest, given = total - most - (amount - 1), [1] * (amount - 1)
    while rest > 0:
        candidates = [i for i in range(amount - 1) if given[i] < most]
        mass, left = sum([weights[i] for i in candidates]), rest
        for i in candidates:
            more = min(most - given[i], max(1, left * weights[i] // mass), rest)
            given[i] = given[i] + more
            rest = rest - more
    return np.array([most] + given)


def uneven_parts(own_key, number_of, total, reach, slope):
    if number_of == 2:
        one = jax.random.randint(own_key, (), max(1, total - reach), min(reach, total - 1) + 1)
        return jnp.stack([one, total - one])
    lengths = jnp.asarray(length_profile(number_of, total, reach, slope), jnp.int32)
    twos = (number_of - 1) // 2
    giver, receiver = lengths[1:1 + 2 * twos:2], lengths[2:2 + 2 * twos:2]
    margin = jnp.minimum(giver - 1, reach - receiver)
    moved = jax.random.randint(jax.random.fold_in(own_key, 1), (twos,), 0, 1 << 20) % (margin + 1)
    lengths = lengths.at[1:1 + 2 * twos:2].set(giver - moved).at[2:2 + 2 * twos:2].set(receiver + moved)
    return lengths[jax.random.permutation(jax.random.fold_in(own_key, 2), number_of)]


def noise(rng, dims, scale, most, held_as=jnp.bfloat16):
    return jnp.clip(scale * jax.random.normal(rng, dims, jnp.float32), -most, most).astype(held_as)


def setup_inputs(seed: int = 0) -> dict:
    key_list = jax.random.split(jax.random.key(seed), 9)
    fields = draw_fields(jax.random.fold_in(key_list[8], 71), 0)
    group_size = uneven_parts(key_list[1], GROUPS, C, GMAX, 2).astype(jnp.int32)
    band_of_row = jnp.searchsorted(jnp.cumsum(uneven_parts(key_list[2], BANDS, NLAT, BAND_MOST, 1)), jnp.arange(NLAT), side="right").astype(jnp.int32)
    basis_spectra = noise(key_list[3], (BANDS, 2 * HALO + 1, NBASIS, 2, FREQ), ((2 * HALO + 1) * NBASIS) ** -0.5, 0.75, jnp.float32)
    basis_coef = noise(key_list[4], (C, NBASIS), 1.0, 5.0, jnp.float32)
    mlp_gain = jnp.clip(1.0 + 0.15 * jax.random.normal(key_list[5], (C,), jnp.float32), 0.25, 1.75)
    w_in = noise(key_list[6], (C, HIDDEN_UNITS), C ** -0.5, 0.25)
    w_out = noise(key_list[7], (HIDDEN_UNITS, C), HIDDEN_UNITS ** -0.5, 0.15625)
    return {"fields": fields, "group_size": group_size, "band_of_row": band_of_row, "basis_spectra": basis_spectra, "basis_coef": basis_coef, "mlp_gain": mlp_gain, "w_in": w_in, "w_out": w_out}


EPSILON = 1e-05

def reference(fields, group_size, band_of_row, basis_spectra, basis_coef, mlp_gain, w_in, w_out):
    values = fields.astype(jnp.float32)
    starts = (jnp.cumsum(group_size) - group_size).astype(jnp.int32)
    channel = jnp.arange(C, dtype=jnp.int32)
    group_of = (lax.optimization_barrier(jnp.sum((channel[:, None] >= starts[None, :]).astype(jnp.int32), axis=1)) - 1).astype(jnp.int32)
    member = (group_of[:, None] == jnp.arange(GROUPS, dtype=jnp.int32)[None, :]).astype(values.dtype)
    counts = group_size.astype(values.dtype) * NLON
    sums = lax.optimization_barrier(jnp.sum(values, axis=1))
    means = jnp.dot(sums, member, precision=lax.Precision.HIGHEST) / counts
    centred = values - jnp.take(means, group_of, axis=1)[:, None, :]
    squares = jnp.dot(lax.optimization_barrier(jnp.sum(centred * centred, axis=1)), member, precision=lax.Precision.HIGHEST) / counts
    scaled = jnp.take(lax.rsqrt(squares + EPSILON), group_of, axis=1)
    normed = centred * scaled[:, None, :]
    spectrum = jnp.fft.rfft(normed, axis=1)
    padding = ((HALO, HALO), (0, 0), (0, 0))
    pad_real = jnp.pad(jnp.real(spectrum), padding)
    pad_imag = jnp.pad(jnp.imag(spectrum), padding)
    taps = 2 * HALO + 1

    def one_row(row_index):
        basis = lax.dynamic_index_in_dim(basis_spectra, band_of_row[row_index], 0, keepdims=False)
        kernel = jnp.einsum('cb,dbpk->dpkc', basis_coef, basis, precision=lax.Precision.HIGHEST)
        win_real = lax.dynamic_slice_in_dim(pad_real, row_index, taps, 0)
        win_imag = lax.dynamic_slice_in_dim(pad_imag, row_index, taps, 0)
        out_real = lax.optimization_barrier(jnp.sum(kernel[:, 0] * win_real - kernel[:, 1] * win_imag, axis=0))
        out_imag = lax.optimization_barrier(jnp.sum(kernel[:, 0] * win_imag + kernel[:, 1] * win_real, axis=0))
        return (out_real, out_imag)
    prod_real, prod_imag = lax.map(one_row, jnp.arange(NLAT, dtype=jnp.int32))
    corr = jnp.fft.irfft(prod_real + 1j * prod_imag, n=NLON, axis=1).astype(values.dtype)
    mixed = (values + corr).astype(jnp.bfloat16)
    mixed = lax.optimization_barrier(mixed)

    def mlp_row(row_block):
        inputs = row_block.astype(jnp.float32)
        centre = lax.optimization_barrier(jnp.mean(inputs, axis=-1, keepdims=True))
        spread = lax.optimization_barrier(jnp.mean((inputs - centre) ** 2, axis=-1, keepdims=True))
        normalised = ((inputs - centre) * lax.rsqrt(spread + EPSILON) * mlp_gain).astype(jnp.bfloat16)
        hidden = jax.nn.gelu(jnp.dot(normalised, w_in, preferred_element_type=jnp.float32), approximate=False).astype(jnp.bfloat16)
        return (inputs + jnp.dot(hidden, w_out, preferred_element_type=jnp.float32)).astype(jnp.bfloat16)
    return lax.map(mlp_row, mixed)
```

```python
import functools
import math

import jax
import jax.numpy as jnp
import numpy as np
from jax import lax
from jax.experimental import pallas as pl
from jax.experimental.pallas import tpu as pltpu
from jax.sharding import PartitionSpec as P

HALO = 4
TAPS = 2 * HALO + 1
EPSILON = 1e-05
AXES = ("lat", "lon")
VMEM = pl.BlockSpec(memory_space=pltpu.VMEM)
SMEM = pl.BlockSpec(memory_space=pltpu.SMEM)
PARAMS = pltpu.CompilerParams(vmem_limit_bytes=60 * 1024 * 1024)


def round_up(value, step):
    return -(-value // step) * step


def dft_tables(lon_count, pieces, width, bins):
    cols = lon_count // pieces
    freq = lon_count // 2 + 1
    phase = np.arange(lon_count)[:, None] * np.arange(freq)[None, :] % lon_count
    angle = phase * (2.0 * math.pi / lon_count)
    cosine = np.cos(angle)
    sine = np.where(2 * phase % lon_count == 0, 0.0, np.sin(angle))
    index = np.arange(freq)
    weight = np.where((index == 0) | (2 * index == lon_count), 1.0, 2.0) / lon_count
    forward = np.zeros((pieces, width, 2, bins), np.float64)
    inverse = np.zeros((pieces, width, 2, bins), np.float64)
    forward[:, :cols, 0, :freq] = cosine.reshape(pieces, cols, freq)
    forward[:, :cols, 1, :freq] = -sine.reshape(pieces, cols, freq)
    inverse[:, :cols, 0, :freq] = (cosine * weight).reshape(pieces, cols, freq)
    inverse[:, :cols, 1, :freq] = (-sine * weight).reshape(pieces, cols, freq)
    forward = forward.reshape(pieces * width, 2 * bins).astype(jnp.bfloat16)
    inverse = inverse.reshape(pieces * width, 2 * bins).T.astype(jnp.bfloat16)
    total = forward.astype(np.float64).sum(axis=0, keepdims=True).astype(np.float32)
    return forward, inverse, total


def kernel_body(coef_ref, basis_ref, out_ref):
    coef = coef_ref[...]

    def step(n, carry):
        basis = basis_ref[n]
        high = basis.astype(jnp.bfloat16)
        low = (basis - high.astype(jnp.float32)).astype(jnp.bfloat16)
        both = jnp.concatenate([high, high, low], axis=0)
        out_ref[n] = jnp.dot(coef, both, preferred_element_type=jnp.float32)
        return carry

    lax.fori_loop(0, basis_ref.shape[0], step, 0, unroll=4)


def corr_body(
    pieces, rows, cols, width, bins,
    band_ref, block_ref, forward_ref, inverse_ref, total_ref, mean_ref, scale_ref, kern_ref,
    out_ref, wide_ref, spec_ref, prod_ref, corr_ref,
):
    chan = block_ref.shape[1]
    bands = block_ref.shape[0] // pieces
    lat = bands * rows
    wide_ref[...] = jnp.zeros_like(wide_ref)
    for band in range(bands):
        for piece in range(pieces):
            cells = block_ref[band * pieces + piece].astype(jnp.float32)
            for row in range(rows):
                at = (band * rows + row) * chan
                wide_ref[at : at + chan, piece * width : piece * width + cols] = cells[
                    :, row * cols : (row + 1) * cols
                ]
    raw = jnp.dot(
        wide_ref[...].astype(jnp.bfloat16), forward_ref[...], preferred_element_type=jnp.float32
    )
    spec_ref[...] = (raw - mean_ref[...] * total_ref[...]) * scale_ref[...]
    for row in range(lat):
        band = band_ref[row]
        real = jnp.zeros((chan, bins), jnp.float32)
        imag = jnp.zeros((chan, bins), jnp.float32)
        for tap in range(TAPS):
            source = row + tap - HALO
            if source < 0 or source >= lat:
                continue
            spec_real = spec_ref[source * chan : (source + 1) * chan, :bins]
            spec_imag = spec_ref[source * chan : (source + 1) * chan, bins:]
            kern_real = kern_ref[band * TAPS + tap, :chan]
            kern_imag = kern_ref[band * TAPS + tap, chan:]
            real = real + kern_real * spec_real - kern_imag * spec_imag
            imag = imag + kern_real * spec_imag + kern_imag * spec_real
        prod_ref[row * chan : (row + 1) * chan, :bins] = real
        prod_ref[row * chan : (row + 1) * chan, bins:] = imag
    corr_ref[...] = jnp.dot(
        prod_ref[...].astype(jnp.bfloat16), inverse_ref[...], preferred_element_type=jnp.float32
    )
    for band in range(bands):
        for piece in range(pieces):
            parts = []
            for row in range(rows):
                at = (band * rows + row) * chan
                parts.append(
                    corr_ref[at : at + chan, piece * width : piece * width + cols]
                )
            cells = block_ref[band * pieces + piece].astype(jnp.float32)
            out_ref[band * pieces + piece] = (
                cells + jnp.concatenate(parts, axis=1)
            ).astype(jnp.bfloat16)


def per_device(fields, group_size, band_of_row, basis_spectra, basis_coef, mlp_gain, w_in, w_out):
    row_count, col_count, chan_count = fields.shape
    pieces = lax.axis_size("lon")
    bands = lax.axis_size("lat")
    devices = pieces * bands
    lon_count = col_count * pieces
    lat_count = row_count * bands
    freq_count = lon_count // 2 + 1
    groups = group_size.shape[0]
    pixels = row_count * col_count
    chan = round_up(-(-chan_count // devices), 8)
    held = devices * chan
    width = round_up(col_count, 128)
    bins = round_up(freq_count, 128)
    band_count, _, basis_count = basis_spectra.shape[:3]
    me = lax.axis_index(AXES)

    turned = jnp.transpose(fields, (2, 0, 1)).reshape(chan_count, pixels)
    turned = jnp.pad(turned, ((0, held - chan_count), (0, 0))).reshape(devices, chan, pixels)
    arrived = lax.all_to_all(turned, AXES, split_axis=0, concat_axis=0, tiled=True)

    starts = jnp.cumsum(group_size) - group_size
    channel = jnp.arange(held, dtype=jnp.int32)
    within = (channel[:, None] >= starts[None, :]) & (
        channel[:, None] < (starts + group_size)[None, :]
    )
    member = within.astype(jnp.float32)
    local = member[:chan_count]
    values = fields.astype(jnp.float32)
    amount = group_size.astype(jnp.float32) * col_count
    centre = (
        jnp.dot(jnp.sum(values, axis=1), local, precision=lax.Precision.HIGHEST) / amount
    )
    middle = jnp.dot(centre, local.T, precision=lax.Precision.HIGHEST)
    offset = values - middle[:, None, :]
    squares = jnp.dot(jnp.sum(offset * offset, axis=1), local, precision=lax.Precision.HIGHEST)
    report = jnp.concatenate(
        [centre.reshape(-1), squares.reshape(-1), band_of_row.astype(jnp.float32)]
    )
    reports = lax.all_gather(report, AXES, axis=0, tiled=False)
    count = row_count * groups
    centres = reports[:, :count].reshape(bands, pieces, row_count, groups)
    spreads = reports[:, count : 2 * count].reshape(bands, pieces, row_count, groups)
    band_rows = reports[:, 2 * count :].reshape(bands, pieces, row_count)[:, 0].reshape(-1)
    band_rows = band_rows.astype(jnp.int32)
    mean = jnp.mean(centres, axis=1)
    total = jnp.sum(spreads + amount * (centres - mean[:, None]) ** 2, axis=1)
    scale = lax.rsqrt(total / (amount * pieces) + EPSILON)
    mine = lax.dynamic_slice_in_dim(member, me * chan, chan, axis=0)
    pick = functools.partial(jnp.einsum, "irg,cg->irc", precision=lax.Precision.HIGHEST)
    mean = pick(mean, mine).reshape(lat_count * chan, 1)
    scale = pick(scale, mine).reshape(lat_count * chan, 1)

    coef = jnp.pad(basis_coef, ((0, held - chan_count), (0, 0)))
    coef = lax.dynamic_slice_in_dim(coef, me * chan, chan, axis=0)
    coef = jnp.einsum("cb,pq->pcbq", coef, jnp.eye(2, dtype=jnp.float32))
    coef = coef.reshape(2 * chan, 2 * basis_count)
    high = coef.astype(jnp.bfloat16)
    low = (coef - high.astype(jnp.float32)).astype(jnp.bfloat16)
    coef = jnp.concatenate([high, low, high], axis=1)
    basis = basis_spectra.reshape(band_count * TAPS, 2 * basis_count, freq_count)
    basis = jnp.pad(basis, ((0, 0), (0, 0), (0, bins - freq_count)))
    kern = pl.pallas_call(
        kernel_body,
        out_shape=jax.ShapeDtypeStruct((band_count * TAPS, 2 * chan, bins), jnp.float32),
        in_specs=[VMEM] * 2,
        out_specs=VMEM,
        compiler_params=PARAMS,
        cost_estimate=pl.CostEstimate(
            flops=2 * 72 * 48 * 48 * 384, bytes_accessed=10_000_000, transcendentals=0
        ),
    )(coef, basis)

    forward, inverse, sums = dft_tables(lon_count, pieces, width, bins)
    mixed = pl.pallas_call(
        functools.partial(corr_body, pieces, row_count, col_count, width, bins),
        out_shape=jax.ShapeDtypeStruct((devices, chan, pixels), jnp.bfloat16),
        in_specs=[SMEM] + [VMEM] * 7,
        out_specs=VMEM,
        scratch_shapes=[
            pltpu.VMEM((lat_count * chan, pieces * width), jnp.float32),
            pltpu.VMEM((lat_count * chan, 2 * bins), jnp.float32),
            pltpu.VMEM((lat_count * chan, 2 * bins), jnp.float32),
            pltpu.VMEM((lat_count * chan, pieces * width), jnp.float32),
        ],
        compiler_params=PARAMS,
    )(band_rows, arrived, forward, inverse, sums, mean, scale, kern)
    returned = lax.all_to_all(mixed, AXES, split_axis=0, concat_axis=0, tiled=True)
    inputs = returned.reshape(held, pixels)[:chan_count].T.astype(jnp.float32)
    centre = jnp.mean(inputs, axis=-1, keepdims=True)
    spread = jnp.mean((inputs - centre) ** 2, axis=-1, keepdims=True)
    normalised = ((inputs - centre) * lax.rsqrt(spread + EPSILON) * mlp_gain).astype(jnp.bfloat16)
    hidden = jax.nn.gelu(
        jnp.dot(normalised, w_in, preferred_element_type=jnp.float32), approximate=False
    ).astype(jnp.bfloat16)
    result = inputs + jnp.dot(hidden, w_out, preferred_element_type=jnp.float32)
    return result.astype(jnp.bfloat16).reshape(row_count, col_count, chan_count)


def solution(mesh):
    placed = (P("lat", "lon", None), P(), P("lat"), P(), P(), P(), P(), P())
    return jax.shard_map(
        per_device, mesh=mesh, in_specs=placed, out_specs=P("lat", "lon", None), check_vma=False
    )
```

```python
import functools
import math

import jax
import jax.numpy as jnp
import numpy as np
from jax import lax
from jax.experimental import pallas as pl
from jax.experimental.pallas import tpu as pltpu
from jax.sharding import PartitionSpec as P

HALO = 4
TAPS = 2 * HALO + 1
EPSILON = 1e-05
VMEM = pl.BlockSpec(memory_space=pltpu.VMEM)
SMEM = pl.BlockSpec(memory_space=pltpu.SMEM)
MESH = pl.DeviceIdType.MESH
DMA = pltpu.SemaphoreType.DMA
PARAMS = pltpu.CompilerParams(vmem_limit_bytes=60 * 1024 * 1024)


def round_up(value, step):
    return -(-value // step) * step


def dft_tables(lon_count, pieces, width, bins):
    cols = lon_count // pieces
    freq = lon_count // 2 + 1
    phase = np.arange(lon_count)[:, None] * np.arange(freq)[None, :] % lon_count
    angle = phase * (2.0 * math.pi / lon_count)
    cosine = np.cos(angle)
    sine = np.where(2 * phase % lon_count == 0, 0.0, np.sin(angle))
    index = np.arange(freq)
    weight = np.where((index == 0) | (2 * index == lon_count), 1.0, 2.0) / lon_count
    table = np.zeros((pieces, width, 2, bins), np.float64)
    table[:, :cols, 0, :freq] = cosine.reshape(pieces, cols, freq)
    table[:, :cols, 1, :freq] = -sine.reshape(pieces, cols, freq)
    table = table.reshape(pieces * width, 2 * bins).astype(jnp.bfloat16)
    total = table.astype(np.float64).sum(axis=0, keepdims=True).astype(np.float32)
    scaled = np.zeros((2, bins), np.float32)
    scaled[:, :freq] = weight
    return table, total, scaled.reshape(1, 2 * bins)


def place(index):
    pieces = lax.axis_size("lon")
    return (lax.div(index, pieces), lax.rem(index, pieces))


def greet(devices, me):
    barrier = pltpu.get_barrier_semaphore()

    def signal(step, carry):
        pl.semaphore_signal(
            barrier, inc=1, device_id=place(lax.rem(me + step, devices)), device_id_type=MESH
        )
        return carry

    lax.fori_loop(1, devices, signal, 0)
    pl.semaphore_wait(barrier, devices - 1)


def own_index():
    return lax.axis_index("lat") * lax.axis_size("lon") + lax.axis_index("lon")


def drain(blocks, amount, semaphore):
    part = blocks.at[pl.ds(0, amount)]
    pltpu.make_async_copy(part, part, semaphore).wait()


def scatter_body(
    devices, active, freq,
    block_ref, report_ref, coef_ref, basis_ref,
    arrived_ref, reports_ref, kern_ref,
    send_sem, recv_sem, report_send_sem, report_recv_sem, local_sem,
):
    me = own_index()
    greet(devices, me)

    def send(step, carry):
        target = lax.rem(me + step, devices)
        pltpu.make_async_remote_copy(
            src_ref=report_ref,
            dst_ref=reports_ref.at[me],
            send_sem=report_send_sem,
            recv_sem=report_recv_sem,
            device_id=place(target),
            device_id_type=MESH,
        ).start()

        @pl.when(target < active)
        def _():
            pltpu.make_async_remote_copy(
                src_ref=block_ref.at[target],
                dst_ref=arrived_ref.at[me],
                send_sem=send_sem,
                recv_sem=recv_sem,
                device_id=place(target),
                device_id_type=MESH,
            ).start()

        return carry

    lax.fori_loop(1, devices, send, 0)
    reports_ref[me] = report_ref[...]
    own = pltpu.make_async_copy(
        block_ref.at[lax.rem(me, active)], arrived_ref.at[me], local_sem
    )
    own.start()

    chan, bins = kern_ref.shape[1] // 2, kern_ref.shape[2]
    coef = coef_ref[...]
    blank = jnp.zeros((basis_ref.shape[1], bins - freq), jnp.float32)

    def generate(n, carry):
        for part in range(2):
            basis = jnp.concatenate([basis_ref[n, :, part, :], blank], axis=1)
            high = basis.astype(jnp.bfloat16).astype(jnp.float32)
            both = jnp.concatenate([high, high, basis - high], axis=0).astype(jnp.bfloat16)
            kern_ref[n, part * chan : (part + 1) * chan] = jnp.dot(
                coef, both, preferred_element_type=jnp.float32
            )
        return carry

    lax.fori_loop(0, basis_ref.shape[0], generate, 0)
    own.wait()
    drain(reports_ref, devices - 1, report_send_sem)
    drain(reports_ref, devices - 1, report_recv_sem)

    @pl.when(me < active)
    def _():
        drain(block_ref, active - 1, send_sem)
        drain(arrived_ref, devices - 1, recv_sem)

    @pl.when(me >= active)
    def _():
        drain(block_ref, active, send_sem)

        def clear(n, carry):
            arrived_ref[n] = jnp.zeros(arrived_ref.shape[1:], arrived_ref.dtype)
            return carry

        lax.fori_loop(0, devices, clear, 0)


def gather_body(devices, active, mixed_ref, returned_ref, send_sem, recv_sem, local_sem):
    me = own_index()
    greet(devices, me)

    @pl.when(me < active)
    def _():
        def send(step, carry):
            target = lax.rem(me + step, devices)
            pltpu.make_async_remote_copy(
                src_ref=mixed_ref.at[target],
                dst_ref=returned_ref.at[me],
                send_sem=send_sem,
                recv_sem=recv_sem,
                device_id=place(target),
                device_id_type=MESH,
            ).start()
            return carry

        lax.fori_loop(1, devices, send, 0)
        own = pltpu.make_async_copy(mixed_ref.at[me], returned_ref.at[me], local_sem)
        own.start()
        own.wait()
        drain(mixed_ref, devices - 1, send_sem)
        drain(returned_ref, active - 1, recv_sem)

    @pl.when(me >= active)
    def _():
        drain(returned_ref, active, recv_sem)


def corr_body(
    pieces, rows, cols, width, bins,
    band_ref, block_ref, table_ref, total_ref, weight_ref, mean_ref, scale_ref, kern_ref,
    out_ref, wide_ref, spec_ref, prod_ref, corr_ref,
):
    chan = block_ref.shape[1]
    bands = block_ref.shape[0] // pieces
    lat = bands * rows
    wide_ref[...] = jnp.zeros_like(wide_ref)
    for band in range(bands):
        for piece in range(pieces):
            cells = block_ref[band * pieces + piece].astype(jnp.float32)
            for row in range(rows):
                at = (band * rows + row) * chan
                wide_ref[at : at + chan, piece * width : piece * width + cols] = cells[
                    :, row * cols : (row + 1) * cols
                ]
    raw = jnp.dot(
        wide_ref[...].astype(jnp.bfloat16), table_ref[...], preferred_element_type=jnp.float32
    )
    spec_ref[...] = (raw - mean_ref[...] * total_ref[...]) * scale_ref[...]
    for row in range(lat):
        band = band_ref[row]
        real = jnp.zeros((chan, bins), jnp.float32)
        imag = jnp.zeros((chan, bins), jnp.float32)
        for tap in range(TAPS):
            source = row + tap - HALO
            if source < 0 or source >= lat:
                continue
            spec_real = spec_ref[source * chan : (source + 1) * chan, :bins]
            spec_imag = spec_ref[source * chan : (source + 1) * chan, bins:]
            kern_real = kern_ref[band * TAPS + tap, :chan]
            kern_imag = kern_ref[band * TAPS + tap, chan:]
            real = real + kern_real * spec_real - kern_imag * spec_imag
            imag = imag + kern_real * spec_imag + kern_imag * spec_real
        prod_ref[row * chan : (row + 1) * chan, :bins] = real
        prod_ref[row * chan : (row + 1) * chan, bins:] = imag
    corr_ref[...] = lax.dot_general(
        (prod_ref[...] * weight_ref[...]).astype(jnp.bfloat16),
        table_ref[...],
        (((1,), (1,)), ((), ())),
        preferred_element_type=jnp.float32,
    )
    for band in range(bands):
        for piece in range(pieces):
            parts = []
            for row in range(rows):
                at = (band * rows + row) * chan
                parts.append(
                    corr_ref[at : at + chan, piece * width : piece * width + cols]
                )
            cells = block_ref[band * pieces + piece].astype(jnp.float32)
            out_ref[band * pieces + piece] = (
                cells + jnp.concatenate(parts, axis=1)
            ).astype(jnp.bfloat16)


def per_device(fields, group_size, band_of_row, basis_spectra, basis_coef, mlp_gain, w_in, w_out):
    row_count, col_count, chan_count = fields.shape
    pieces = lax.axis_size("lon")
    bands = lax.axis_size("lat")
    devices = pieces * bands
    lon_count = col_count * pieces
    lat_count = row_count * bands
    freq_count = lon_count // 2 + 1
    groups = group_size.shape[0]
    pixels = row_count * col_count
    chan = round_up(-(-chan_count // devices), 8)
    held = devices * chan
    active = -(-chan_count // chan)
    width = round_up(col_count, 128)
    bins = round_up(freq_count, 128)
    band_count, _, basis_count = basis_spectra.shape[:3]
    me = own_index()

    turned = jnp.transpose(fields, (2, 0, 1)).reshape(chan_count, pixels)
    turned = jnp.pad(turned, ((0, active * chan - chan_count), (0, 0)))
    turned = turned.reshape(active, chan, pixels)

    starts = jnp.cumsum(group_size) - group_size
    channel = jnp.arange(held, dtype=jnp.int32)
    within = (channel[:, None] >= starts[None, :]) & (
        channel[:, None] < (starts + group_size)[None, :]
    )
    member = within.astype(jnp.float32)
    local = member[:chan_count]
    values = fields.astype(jnp.float32)
    amount = group_size.astype(jnp.float32) * col_count
    centre = (
        jnp.dot(jnp.sum(values, axis=1), local, precision=lax.Precision.HIGHEST) / amount
    )
    middle = jnp.dot(centre, local.T, precision=lax.Precision.HIGHEST)
    offset = values - middle[:, None, :]
    squares = jnp.dot(jnp.sum(offset * offset, axis=1), local, precision=lax.Precision.HIGHEST)
    count = row_count * groups
    report = jnp.concatenate(
        [centre.reshape(-1), squares.reshape(-1), band_of_row.astype(jnp.float32)]
    )
    report = jnp.pad(report, (0, round_up(report.shape[0], 128) - report.shape[0])).reshape(1, -1)

    coef = jnp.pad(basis_coef, ((0, held - chan_count), (0, 0)))
    coef = lax.dynamic_slice_in_dim(coef, me * chan, chan, axis=0)
    high = coef.astype(jnp.bfloat16)
    low = (coef - high.astype(jnp.float32)).astype(jnp.bfloat16)
    coef = jnp.concatenate([high, low, high], axis=1)
    basis = basis_spectra.reshape(band_count * TAPS, basis_count, 2, freq_count)
    arrived, reports, kern = pl.pallas_call(
        functools.partial(scatter_body, devices, active, freq_count),
        out_shape=[
            jax.ShapeDtypeStruct((devices, chan, pixels), jnp.bfloat16),
            jax.ShapeDtypeStruct((devices, 1, report.shape[1]), jnp.float32),
            jax.ShapeDtypeStruct((band_count * TAPS, 2 * chan, bins), jnp.float32),
        ],
        in_specs=[VMEM] * 4,
        out_specs=[VMEM] * 3,
        scratch_shapes=[DMA] * 5,
        compiler_params=pltpu.CompilerParams(
            collective_id=0, has_side_effects=True, vmem_limit_bytes=60 * 1024 * 1024
        ),
    )(turned, report, coef, basis)
    reports = reports[:, 0]
    centres = reports[:, :count].reshape(bands, pieces, row_count, groups)
    spreads = reports[:, count : 2 * count].reshape(bands, pieces, row_count, groups)
    band_rows = reports[:, 2 * count : 2 * count + row_count]
    band_rows = band_rows.reshape(bands, pieces, row_count)[:, 0].reshape(-1).astype(jnp.int32)
    mean = jnp.mean(centres, axis=1)
    total = jnp.sum(spreads + amount * (centres - mean[:, None]) ** 2, axis=1)
    scale = lax.rsqrt(total / (amount * pieces) + EPSILON)
    mine = lax.dynamic_slice_in_dim(member, me * chan, chan, axis=0)
    pick = functools.partial(jnp.einsum, "irg,cg->irc", precision=lax.Precision.HIGHEST)
    mean = pick(mean, mine).reshape(lat_count * chan, 1)
    scale = pick(scale, mine).reshape(lat_count * chan, 1)

    table, sums, weight = dft_tables(lon_count, pieces, width, bins)
    mixed = pl.pallas_call(
        functools.partial(corr_body, pieces, row_count, col_count, width, bins),
        out_shape=jax.ShapeDtypeStruct((devices, chan, pixels), jnp.bfloat16),
        in_specs=[SMEM] + [VMEM] * 7,
        out_specs=VMEM,
        scratch_shapes=[
            pltpu.VMEM((lat_count * chan, pieces * width), jnp.float32),
            pltpu.VMEM((lat_count * chan, 2 * bins), jnp.float32),
            pltpu.VMEM((lat_count * chan, 2 * bins), jnp.float32),
            pltpu.VMEM((lat_count * chan, pieces * width), jnp.float32),
        ],
        compiler_params=PARAMS,
    )(band_rows, arrived, table, sums, weight, mean, scale, kern)
    returned = pl.pallas_call(
        functools.partial(gather_body, devices, active),
        out_shape=jax.ShapeDtypeStruct((active, chan, pixels), jnp.bfloat16),
        in_specs=[VMEM],
        out_specs=VMEM,
        scratch_shapes=[DMA] * 3,
        compiler_params=pltpu.CompilerParams(
            collective_id=1, has_side_effects=True, vmem_limit_bytes=60 * 1024 * 1024
        ),
    )(mixed)
    inputs = returned.reshape(active * chan, pixels)[:chan_count].T.astype(jnp.float32)
    centre = jnp.mean(inputs, axis=-1, keepdims=True)
    spread = jnp.mean((inputs - centre) ** 2, axis=-1, keepdims=True)
    normalised = ((inputs - centre) * lax.rsqrt(spread + EPSILON) * mlp_gain).astype(jnp.bfloat16)
    hidden = jax.nn.gelu(
        jnp.dot(normalised, w_in, preferred_element_type=jnp.float32), approximate=False
    ).astype(jnp.bfloat16)
    result = inputs + jnp.dot(hidden, w_out, preferred_element_type=jnp.float32)
    return result.astype(jnp.bfloat16).reshape(row_count, col_count, chan_count)


def solution(mesh):
    placed = (P("lat", "lon", None), P(), P("lat"), P(), P(), P(), P(), P())
    return jax.shard_map(
        per_device, mesh=mesh, in_specs=placed, out_specs=P("lat", "lon", None), check_vma=False
    )
```

```python
import functools
import math

import jax
import jax.numpy as jnp
import numpy as np
from jax import lax
from jax.experimental import pallas as pl
from jax.experimental.pallas import tpu as pltpu
from jax.sharding import PartitionSpec as P

HALO = 4
TAPS = 2 * HALO + 1
EPSILON = 1e-05
VMEM = pl.BlockSpec(memory_space=pltpu.VMEM)
SMEM = pl.BlockSpec(memory_space=pltpu.SMEM)
MESH = pl.DeviceIdType.MESH
DMA = pltpu.SemaphoreType.DMA
PARAMS = pltpu.CompilerParams(vmem_limit_bytes=60 * 1024 * 1024)


def round_up(value, step):
    return -(-value // step) * step


def dft_tables(lon_count, pieces, width, bins):
    cols = lon_count // pieces
    freq = lon_count // 2 + 1
    phase = np.arange(lon_count)[:, None] * np.arange(freq)[None, :] % lon_count
    angle = phase * (2.0 * math.pi / lon_count)
    cosine = np.cos(angle)
    sine = np.where(2 * phase % lon_count == 0, 0.0, np.sin(angle))
    index = np.arange(freq)
    weight = np.where((index == 0) | (2 * index == lon_count), 1.0, 2.0) / lon_count
    table = np.zeros((pieces, width, 2, bins), np.float64)
    table[:, :cols, 0, :freq] = cosine.reshape(pieces, cols, freq)
    table[:, :cols, 1, :freq] = -sine.reshape(pieces, cols, freq)
    table = table.reshape(pieces * width, 2 * bins).astype(jnp.bfloat16)
    total = table.astype(np.float64).sum(axis=0, keepdims=True).astype(np.float32)
    scaled = np.zeros((2, bins), np.float32)
    scaled[:, :freq] = weight
    return table, total, scaled.reshape(1, 2 * bins)


def place(index):
    pieces = lax.axis_size("lon")
    return (lax.div(index, pieces), lax.rem(index, pieces))


def greet(devices, me):
    barrier = pltpu.get_barrier_semaphore()

    def signal(step, carry):
        pl.semaphore_signal(
            barrier, inc=1, device_id=place(lax.rem(me + step, devices)), device_id_type=MESH
        )
        return carry

    lax.fori_loop(1, devices, signal, 0)
    pl.semaphore_wait(barrier, devices - 1)


def own_index():
    return lax.axis_index("lat") * lax.axis_size("lon") + lax.axis_index("lon")


def drain(blocks, amount, semaphore):
    part = blocks.at[pl.ds(0, amount)]
    pltpu.make_async_copy(part, part, semaphore).wait()


def group_rows(size_ref, lanes, groups):
    group = lax.rem(lax.broadcasted_iota(jnp.int32, (1, lanes), 1), groups)
    start = jnp.zeros((1, lanes), jnp.int32)
    size = jnp.zeros((1, lanes), jnp.int32)
    for index in range(groups):
        start = start + jnp.where(group > index, size_ref[index], 0)
        size = size + jnp.where(group == index, size_ref[index], 0)
    return start, size


def membership(first, chan, start, size):
    channel = first + lax.broadcasted_iota(jnp.int32, (chan, start.shape[1]), 0)
    return (channel >= start) & (channel < start + size)


def scatter_body(
    devices, active, freq, rows, cols, groups,
    size_ref, band_ref, block_ref, coef_ref, basis_ref,
    arrived_ref, reports_ref, kern_ref,
    mean_ref, square_ref, report_ref,
    send_sem, recv_sem, report_send_sem, report_recv_sem, local_sem,
):
    me = own_index()
    greet(devices, me)

    def send(step, carry):
        target = lax.rem(me + step, devices)

        @pl.when(target < active)
        def _():
            pltpu.make_async_remote_copy(
                src_ref=block_ref.at[target],
                dst_ref=arrived_ref.at[me],
                send_sem=send_sem,
                recv_sem=recv_sem,
                device_id=place(target),
                device_id_type=MESH,
            ).start()

        return carry

    lax.fori_loop(1, devices, send, 0)
    own = pltpu.make_async_copy(
        block_ref.at[lax.rem(me, active)], arrived_ref.at[me], local_sem
    )
    own.start()

    chan = block_ref.shape[1]
    lane = lax.broadcasted_iota(jnp.int32, (chan, block_ref.shape[2]), 1)
    slot = lax.broadcasted_iota(jnp.int32, (chan, 128), 1)

    def measure(n, carry):
        cells = block_ref[n].astype(jnp.float32)
        means = jnp.zeros((chan, 128), jnp.float32)
        squares = jnp.zeros((chan, 128), jnp.float32)
        for row in range(rows):
            inside = (lane >= row * cols) & (lane < (row + 1) * cols)
            mean = jnp.sum(jnp.where(inside, cells, 0.0), axis=1, keepdims=True) / cols
            offset = jnp.where(inside, cells - mean, 0.0)
            square = jnp.sum(offset * offset, axis=1, keepdims=True)
            means = jnp.where(slot == row, mean, means)
            squares = jnp.where(slot == row, square, squares)
        at = pl.multiple_of(n * chan, 8)
        mean_ref[pl.ds(at, chan)] = means
        square_ref[pl.ds(at, chan)] = squares
        return carry

    lax.fori_loop(0, active, measure, 0)
    exact = functools.partial(
        lax.dot_general, precision=lax.Precision.HIGHEST, preferred_element_type=jnp.float32
    )
    over_chan = (((0,), (0,)), ((), ()))
    over_last = (((1,), (1,)), ((), ()))
    start, size = group_rows(size_ref, 128, groups)
    member = jnp.where(
        membership(0, active * chan, start, size)
        & (lax.broadcasted_iota(jnp.int32, (1, 128), 1) < groups),
        1.0, 0.0,
    )
    means = mean_ref[...]
    centre = exact(means, member, over_chan) / jnp.maximum(size, 1).astype(jnp.float32)
    offset = means - exact(member, centre, over_last)
    spread = exact(square_ref[...] + cols * offset * offset, member, over_chan)
    rest = report_ref.shape[1] - 2 * rows * groups
    place_of = lax.broadcasted_iota(jnp.int32, (1, rest), 1)
    bands = jnp.zeros((1, rest), jnp.float32)
    for row in range(rows):
        bands = jnp.where(place_of == row, band_ref[row].astype(jnp.float32), bands)
    report = jnp.concatenate(
        [centre[row : row + 1, :groups] for row in range(rows)]
        + [spread[row : row + 1, :groups] for row in range(rows)]
        + [bands],
        axis=1,
    )
    report_ref[...] = report
    reports_ref[me] = report

    bins = kern_ref.shape[2]
    total = coef_ref.shape[1]
    wanted = me * chan + lax.broadcasted_iota(jnp.int32, (chan, total), 0)
    chosen = jnp.where(lax.broadcasted_iota(jnp.int32, (chan, total), 1) == wanted, 1.0, 0.0)
    coef = exact(chosen, coef_ref[...], over_last)
    high = coef.astype(jnp.bfloat16).astype(jnp.float32)
    coef = jnp.concatenate([high, coef - high, high], axis=1).astype(jnp.bfloat16)
    blank = jnp.zeros((basis_ref.shape[1], bins - freq), jnp.float32)

    def generate(n, carry):
        for part in range(2):
            basis = jnp.concatenate([basis_ref[n, :, part, :], blank], axis=1)
            high = basis.astype(jnp.bfloat16).astype(jnp.float32)
            both = jnp.concatenate([high, high, basis - high], axis=0).astype(jnp.bfloat16)
            kern_ref[n, part * chan : (part + 1) * chan] = jnp.dot(
                coef, both, preferred_element_type=jnp.float32
            )
        return carry

    def tell(step, carry):
        pltpu.make_async_remote_copy(
            src_ref=report_ref,
            dst_ref=reports_ref.at[me],
            send_sem=report_send_sem,
            recv_sem=report_recv_sem,
            device_id=place(lax.rem(me + step, devices)),
            device_id_type=MESH,
        ).start()
        return carry

    early = basis_ref.shape[0] // 8
    lax.fori_loop(0, early, generate, 0)
    lax.fori_loop(1, devices, tell, 0)
    lax.fori_loop(early, basis_ref.shape[0], generate, 0)
    own.wait()
    drain(reports_ref, devices - 1, report_send_sem)
    drain(reports_ref, devices - 1, report_recv_sem)

    @pl.when(me < active)
    def _():
        drain(block_ref, active - 1, send_sem)
        drain(arrived_ref, devices - 1, recv_sem)

    @pl.when(me >= active)
    def _():
        drain(block_ref, active, send_sem)

        def clear(n, carry):
            arrived_ref[n] = jnp.zeros(arrived_ref.shape[1:], arrived_ref.dtype)
            return carry

        lax.fori_loop(0, devices, clear, 0)


def gather_body(devices, active, mixed_ref, returned_ref, send_sem, recv_sem, local_sem):
    me = own_index()
    greet(devices, me)

    @pl.when(me < active)
    def _():
        def send(step, carry):
            target = lax.rem(me + step, devices)
            pltpu.make_async_remote_copy(
                src_ref=mixed_ref.at[target],
                dst_ref=returned_ref.at[me],
                send_sem=send_sem,
                recv_sem=recv_sem,
                device_id=place(target),
                device_id_type=MESH,
            ).start()
            return carry

        lax.fori_loop(1, devices, send, 0)
        own = pltpu.make_async_copy(mixed_ref.at[me], returned_ref.at[me], local_sem)
        own.start()
        own.wait()
        drain(mixed_ref, devices - 1, send_sem)
        drain(returned_ref, active - 1, recv_sem)

    @pl.when(me >= active)
    def _():
        drain(returned_ref, active, recv_sem)


def corr_body(
    pieces, rows, cols, width, bins, groups,
    size_ref, block_ref, reports_ref, table_ref, total_ref, weight_ref, kern_ref,
    out_ref, wide_ref, spec_ref, prod_ref, corr_ref,
):
    chan = block_ref.shape[1]
    bands = block_ref.shape[0] // pieces
    lat = bands * rows
    lanes = reports_ref.shape[2]
    start, size = group_rows(size_ref, lanes, groups)
    amount = size.astype(jnp.float32) * cols
    lane = lax.broadcasted_iota(jnp.int32, (1, lanes), 1)
    member = membership(own_index() * chan, chan, start, size)
    means, scales, numbers = [], [], []
    for band in range(bands):
        report = reports_ref[band * pieces : (band + 1) * pieces, 0]
        centre = jnp.sum(report, axis=0, keepdims=True) / pieces
        offset = report - centre
        between = amount * jnp.sum(offset * offset, axis=0, keepdims=True)
        within = jnp.sum(report, axis=0, keepdims=True)
        for row in range(rows):
            low, high = row * groups, (rows + row) * groups
            here = member & (lane >= low) & (lane < low + groups)
            there = member & (lane >= high) & (lane < high + groups)

            def pick(mask, cells):
                return jnp.sum(jnp.where(mask, cells, 0.0), axis=1, keepdims=True)

            square = pick(here, between) + pick(there, within)
            count = pick(here, amount) * pieces
            means.append(pick(here, centre))
            scales.append(lax.rsqrt(square / jnp.maximum(count, 1.0) + EPSILON))
            mark = lane == 2 * rows * groups + row
            numbers.append(jnp.sum(jnp.where(mark, report[:1], 0.0)).astype(jnp.int32))
    wide_ref[...] = jnp.zeros_like(wide_ref)
    for band in range(bands):
        for piece in range(pieces):
            cells = block_ref[band * pieces + piece].astype(jnp.float32)
            for row in range(rows):
                at = (band * rows + row) * chan
                wide_ref[at : at + chan, piece * width : piece * width + cols] = cells[
                    :, row * cols : (row + 1) * cols
                ]
    raw = jnp.dot(
        wide_ref[...].astype(jnp.bfloat16), table_ref[...], preferred_element_type=jnp.float32
    )
    for row in range(lat):
        at = row * chan
        spec_ref[at : at + chan] = (raw[at : at + chan] - means[row] * total_ref[...]) * scales[row]
    for row in range(lat):
        band = numbers[row]
        real = jnp.zeros((chan, bins), jnp.float32)
        imag = jnp.zeros((chan, bins), jnp.float32)
        for tap in range(TAPS):
            source = row + tap - HALO
            if source < 0 or source >= lat:
                continue
            spec_real = spec_ref[source * chan : (source + 1) * chan, :bins]
            spec_imag = spec_ref[source * chan : (source + 1) * chan, bins:]
            kern_real = kern_ref[band * TAPS + tap, :chan]
            kern_imag = kern_ref[band * TAPS + tap, chan:]
            real = real + kern_real * spec_real - kern_imag * spec_imag
            imag = imag + kern_real * spec_imag + kern_imag * spec_real
        prod_ref[row * chan : (row + 1) * chan, :bins] = real
        prod_ref[row * chan : (row + 1) * chan, bins:] = imag
    corr_ref[...] = lax.dot_general(
        (prod_ref[...] * weight_ref[...]).astype(jnp.bfloat16),
        table_ref[...],
        (((1,), (1,)), ((), ())),
        preferred_element_type=jnp.float32,
    )
    for band in range(bands):
        for piece in range(pieces):
            parts = []
            for row in range(rows):
                at = (band * rows + row) * chan
                parts.append(
                    corr_ref[at : at + chan, piece * width : piece * width + cols]
                )
            cells = block_ref[band * pieces + piece].astype(jnp.float32)
            out_ref[band * pieces + piece] = (
                cells + jnp.concatenate(parts, axis=1)
            ).astype(jnp.bfloat16)


def per_device(fields, group_size, band_of_row, basis_spectra, basis_coef, mlp_gain, w_in, w_out):
    row_count, col_count, chan_count = fields.shape
    pieces = lax.axis_size("lon")
    bands = lax.axis_size("lat")
    devices = pieces * bands
    lon_count = col_count * pieces
    lat_count = row_count * bands
    freq_count = lon_count // 2 + 1
    groups = group_size.shape[0]
    pixels = row_count * col_count
    chan = round_up(-(-chan_count // devices), 8)
    active = -(-chan_count // chan)
    width = round_up(col_count, 128)
    bins = round_up(freq_count, 128)
    band_count, _, basis_count = basis_spectra.shape[:3]

    turned = jnp.transpose(fields, (2, 0, 1)).reshape(chan_count, pixels)
    turned = jnp.pad(turned, ((0, active * chan - chan_count), (0, 0)))
    turned = turned.reshape(active, chan, pixels)

    lanes = round_up((2 * groups + 1) * row_count, 128)
    basis = basis_spectra.reshape(band_count * TAPS, basis_count, 2, freq_count)
    arrived, reports, kern = pl.pallas_call(
        functools.partial(
            scatter_body, devices, active, freq_count, row_count, col_count, groups
        ),
        out_shape=[
            jax.ShapeDtypeStruct((devices, chan, pixels), jnp.bfloat16),
            jax.ShapeDtypeStruct((devices, 1, lanes), jnp.float32),
            jax.ShapeDtypeStruct((band_count * TAPS, 2 * chan, bins), jnp.float32),
        ],
        in_specs=[SMEM] * 2 + [VMEM] * 3,
        out_specs=[VMEM] * 3,
        scratch_shapes=[
            pltpu.VMEM((active * chan, 128), jnp.float32),
            pltpu.VMEM((active * chan, 128), jnp.float32),
            pltpu.VMEM((1, lanes), jnp.float32),
        ]
        + [DMA] * 5,
        compiler_params=pltpu.CompilerParams(
            collective_id=0, has_side_effects=True, vmem_limit_bytes=60 * 1024 * 1024
        ),
    )(group_size, band_of_row, turned, basis_coef.T, basis)
    table, sums, weight = dft_tables(lon_count, pieces, width, bins)
    mixed = pl.pallas_call(
        functools.partial(corr_body, pieces, row_count, col_count, width, bins, groups),
        out_shape=jax.ShapeDtypeStruct((devices, chan, pixels), jnp.bfloat16),
        in_specs=[SMEM] + [VMEM] * 6,
        out_specs=VMEM,
        scratch_shapes=[
            pltpu.VMEM((lat_count * chan, pieces * width), jnp.float32),
            pltpu.VMEM((lat_count * chan, 2 * bins), jnp.float32),
            pltpu.VMEM((lat_count * chan, 2 * bins), jnp.float32),
            pltpu.VMEM((lat_count * chan, pieces * width), jnp.float32),
        ],
        compiler_params=PARAMS,
    )(group_size, arrived, reports, table, sums, weight, kern)
    returned = pl.pallas_call(
        functools.partial(gather_body, devices, active),
        out_shape=jax.ShapeDtypeStruct((active, chan, pixels), jnp.bfloat16),
        in_specs=[VMEM],
        out_specs=VMEM,
        scratch_shapes=[DMA] * 3,
        compiler_params=pltpu.CompilerParams(
            collective_id=1, has_side_effects=True, vmem_limit_bytes=60 * 1024 * 1024
        ),
    )(mixed)
    inputs = returned.reshape(active * chan, pixels)[:chan_count].T.astype(jnp.float32)
    centre = jnp.mean(inputs, axis=-1, keepdims=True)
    spread = jnp.mean((inputs - centre) ** 2, axis=-1, keepdims=True)
    normalised = ((inputs - centre) * lax.rsqrt(spread + EPSILON) * mlp_gain).astype(jnp.bfloat16)
    hidden = jax.nn.gelu(
        jnp.dot(normalised, w_in, preferred_element_type=jnp.float32), approximate=False
    ).astype(jnp.bfloat16)
    result = inputs + jnp.dot(hidden, w_out, preferred_element_type=jnp.float32)
    return result.astype(jnp.bfloat16).reshape(row_count, col_count, chan_count)


def solution(mesh):
    placed = (P("lat", "lon", None), P(), P("lat"), P(), P(), P(), P(), P())
    return jax.shard_map(
        per_device, mesh=mesh, in_specs=placed, out_specs=P("lat", "lon", None), check_vma=False
    )
```

```python
import functools
import math

import jax
import jax.numpy as jnp
import numpy as np
from jax import lax
from jax.experimental import pallas as pl
from jax.experimental.pallas import tpu as pltpu
from jax.sharding import PartitionSpec as P

HALO = 4
TAPS = 2 * HALO + 1
EPSILON = 1e-05
VMEM = pl.BlockSpec(memory_space=pltpu.VMEM)
SMEM = pl.BlockSpec(memory_space=pltpu.SMEM)
MESH = pl.DeviceIdType.MESH
DMA = pltpu.SemaphoreType.DMA
PARAMS = pltpu.CompilerParams(vmem_limit_bytes=60 * 1024 * 1024)


def round_up(value, step):
    return -(-value // step) * step


def dft_tables(lon_count, pieces, width, bins):
    cols = lon_count // pieces
    freq = lon_count // 2 + 1
    phase = np.arange(lon_count)[:, None] * np.arange(freq)[None, :] % lon_count
    angle = phase * (2.0 * math.pi / lon_count)
    cosine = np.cos(angle)
    sine = np.where(2 * phase % lon_count == 0, 0.0, np.sin(angle))
    index = np.arange(freq)
    weight = np.where((index == 0) | (2 * index == lon_count), 1.0, 2.0) / lon_count
    table = np.zeros((pieces, width, 2, bins), np.float64)
    table[:, :cols, 0, :freq] = cosine.reshape(pieces, cols, freq)
    table[:, :cols, 1, :freq] = -sine.reshape(pieces, cols, freq)
    table = table.reshape(pieces * width, 2 * bins).astype(jnp.bfloat16)
    total = table.astype(np.float64).sum(axis=0, keepdims=True).astype(np.float32)
    scaled = np.zeros((2, bins), np.float32)
    scaled[:, :freq] = weight
    return table, total, scaled.reshape(1, 2 * bins)


def place(index):
    pieces = lax.axis_size("lon")
    return (lax.div(index, pieces), lax.rem(index, pieces))


def greet(devices, me):
    barrier = pltpu.get_barrier_semaphore()

    def signal(step, carry):
        pl.semaphore_signal(
            barrier, inc=1, device_id=place(lax.rem(me + step, devices)), device_id_type=MESH
        )
        return carry

    lax.fori_loop(1, devices, signal, 0)
    pl.semaphore_wait(barrier, devices - 1)


def own_index():
    return lax.axis_index("lat") * lax.axis_size("lon") + lax.axis_index("lon")


def drain(blocks, amount, semaphore):
    part = blocks.at[pl.ds(0, amount)]
    pltpu.make_async_copy(part, part, semaphore).wait()


def group_rows(size_ref, lanes, groups):
    group = lax.rem(lax.broadcasted_iota(jnp.int32, (1, lanes), 1), groups)
    start = jnp.zeros((1, lanes), jnp.int32)
    size = jnp.zeros((1, lanes), jnp.int32)
    for index in range(groups):
        start = start + jnp.where(group > index, size_ref[index], 0)
        size = size + jnp.where(group == index, size_ref[index], 0)
    return start, size


def membership(first, chan, start, size):
    channel = first + lax.broadcasted_iota(jnp.int32, (chan, start.shape[1]), 0)
    return (channel >= start) & (channel < start + size)


def scatter_body(
    devices, active, freq, rows, cols, groups,
    size_ref, band_ref, block_ref, flat_ref, coef_ref, basis_ref,
    arrived_ref, reports_ref, kern_ref,
    report_ref,
    send_sem, recv_sem, report_send_sem, report_recv_sem, local_sem,
):
    me = own_index()
    greet(devices, me)

    def send(step, carry):
        target = lax.rem(me + step, devices)

        @pl.when(target < active)
        def _():
            pltpu.make_async_remote_copy(
                src_ref=block_ref.at[target],
                dst_ref=arrived_ref.at[me],
                send_sem=send_sem,
                recv_sem=recv_sem,
                device_id=place(target),
                device_id_type=MESH,
            ).start()

        return carry

    lax.fori_loop(1, devices, send, 0)
    own = pltpu.make_async_copy(
        block_ref.at[lax.rem(me, active)], arrived_ref.at[me], local_sem
    )
    own.start()

    chan = block_ref.shape[1]
    pixels = rows * cols
    lane = lax.broadcasted_iota(jnp.int32, (pixels, 128), 0)
    slot = lax.broadcasted_iota(jnp.int32, (pixels, 128), 1)
    segment = (lane >= slot * cols) & (lane < (slot + 1) * cols)
    segment = jnp.where(segment, 1.0, 0.0).astype(jnp.bfloat16)

    def add_up(cells):
        return jnp.dot(cells, segment, preferred_element_type=jnp.float32)

    cells = flat_ref[...]
    means = add_up(cells) / cols
    near = means.astype(jnp.bfloat16)
    spread_out = lax.dot_general(
        near, segment, (((1,), (1,)), ((), ())), preferred_element_type=jnp.float32
    )
    offset = cells.astype(jnp.float32) - spread_out
    square = offset * offset
    high = square.astype(jnp.bfloat16)
    low = (square - high.astype(jnp.float32)).astype(jnp.bfloat16)
    shift = means - near.astype(jnp.float32)
    squares = jnp.maximum(add_up(high) + add_up(low) - cols * shift * shift, 0.0)
    exact = functools.partial(
        lax.dot_general, precision=lax.Precision.HIGHEST, preferred_element_type=jnp.float32
    )
    over_chan = (((0,), (0,)), ((), ()))
    over_last = (((1,), (1,)), ((), ()))
    start, size = group_rows(size_ref, 128, groups)
    member = jnp.where(
        membership(0, active * chan, start, size)
        & (lax.broadcasted_iota(jnp.int32, (1, 128), 1) < groups),
        1.0, 0.0,
    )
    centre = exact(means, member, over_chan) / jnp.maximum(size, 1).astype(jnp.float32)
    offset = means - exact(member, centre, over_last)
    spread = exact(squares + cols * offset * offset, member, over_chan)
    rest = report_ref.shape[1] - 2 * rows * groups
    place_of = lax.broadcasted_iota(jnp.int32, (1, rest), 1)
    bands = jnp.zeros((1, rest), jnp.float32)
    for row in range(rows):
        bands = jnp.where(place_of == row, band_ref[row].astype(jnp.float32), bands)
    report = jnp.concatenate(
        [centre[row : row + 1, :groups] for row in range(rows)]
        + [spread[row : row + 1, :groups] for row in range(rows)]
        + [bands],
        axis=1,
    )
    report_ref[...] = report
    reports_ref[me] = report

    bins = kern_ref.shape[2]
    total = coef_ref.shape[1]
    wanted = me * chan + lax.broadcasted_iota(jnp.int32, (chan, total), 0)
    chosen = jnp.where(lax.broadcasted_iota(jnp.int32, (chan, total), 1) == wanted, 1.0, 0.0)
    coef = exact(chosen, coef_ref[...], over_last)
    high = coef.astype(jnp.bfloat16).astype(jnp.float32)
    coef = jnp.concatenate([high, coef - high, high], axis=1).astype(jnp.bfloat16)
    blank = jnp.zeros((basis_ref.shape[1], bins - freq), jnp.float32)

    def generate(n, carry):
        basis = jnp.concatenate(
            [basis_ref[n, :, 0, :], blank, basis_ref[n, :, 1, :], blank], axis=1
        )
        high = basis.astype(jnp.bfloat16).astype(jnp.float32)
        both = jnp.concatenate([high, high, basis - high], axis=0).astype(jnp.bfloat16)
        made = jnp.dot(coef, both, preferred_element_type=jnp.float32)
        kern_ref[n, :chan] = made[:, :bins]
        kern_ref[n, chan:] = made[:, bins:]
        return carry

    def tell(step, carry):
        pltpu.make_async_remote_copy(
            src_ref=report_ref,
            dst_ref=reports_ref.at[me],
            send_sem=report_send_sem,
            recv_sem=report_recv_sem,
            device_id=place(lax.rem(me + step, devices)),
            device_id_type=MESH,
        ).start()
        return carry

    early = basis_ref.shape[0] // 8
    lax.fori_loop(0, early, generate, 0, unroll=3)
    lax.fori_loop(1, devices, tell, 0)
    lax.fori_loop(early, basis_ref.shape[0], generate, 0, unroll=3)
    own.wait()
    drain(reports_ref, devices - 1, report_send_sem)
    drain(reports_ref, devices - 1, report_recv_sem)

    @pl.when(me < active)
    def _():
        drain(block_ref, active - 1, send_sem)
        drain(arrived_ref, devices - 1, recv_sem)

    @pl.when(me >= active)
    def _():
        drain(block_ref, active, send_sem)

        def clear(n, carry):
            arrived_ref[n] = jnp.zeros(arrived_ref.shape[1:], arrived_ref.dtype)
            return carry

        lax.fori_loop(0, devices, clear, 0)


def gather_body(devices, active, mixed_ref, returned_ref, send_sem, recv_sem, local_sem):
    me = own_index()
    greet(devices, me)

    @pl.when(me < active)
    def _():
        def send(step, carry):
            target = lax.rem(me + step, devices)
            pltpu.make_async_remote_copy(
                src_ref=mixed_ref.at[target],
                dst_ref=returned_ref.at[me],
                send_sem=send_sem,
                recv_sem=recv_sem,
                device_id=place(target),
                device_id_type=MESH,
            ).start()
            return carry

        lax.fori_loop(1, devices, send, 0)
        own = pltpu.make_async_copy(mixed_ref.at[me], returned_ref.at[me], local_sem)
        own.start()
        own.wait()
        drain(mixed_ref, devices - 1, send_sem)
        drain(returned_ref, active - 1, recv_sem)

    @pl.when(me >= active)
    def _():
        drain(returned_ref, active, recv_sem)


def corr_body(
    pieces, rows, cols, width, bins, groups,
    size_ref, block_ref, reports_ref, table_ref, total_ref, weight_ref, kern_ref,
    out_ref, wide_ref, spec_ref, prod_ref, corr_ref,
):
    chan = block_ref.shape[1]
    bands = block_ref.shape[0] // pieces
    lat = bands * rows
    lanes = reports_ref.shape[2]
    start, size = group_rows(size_ref, lanes, groups)
    amount = size.astype(jnp.float32) * cols
    lane = lax.broadcasted_iota(jnp.int32, (1, lanes), 1)
    member = membership(own_index() * chan, chan, start, size)
    means, scales, numbers = [], [], []
    for band in range(bands):
        report = reports_ref[band * pieces : (band + 1) * pieces, 0]
        centre = jnp.sum(report, axis=0, keepdims=True) / pieces
        offset = report - centre
        between = amount * jnp.sum(offset * offset, axis=0, keepdims=True)
        within = jnp.sum(report, axis=0, keepdims=True)
        for row in range(rows):
            low, high = row * groups, (rows + row) * groups
            here = member & (lane >= low) & (lane < low + groups)
            there = member & (lane >= high) & (lane < high + groups)

            def pick(mask, cells):
                return jnp.sum(jnp.where(mask, cells, 0.0), axis=1, keepdims=True)

            square = pick(here, between) + pick(there, within)
            count = pick(here, amount) * pieces
            means.append(pick(here, centre))
            scales.append(lax.rsqrt(square / jnp.maximum(count, 1.0) + EPSILON))
            mark = lane == 2 * rows * groups + row
            numbers.append(jnp.sum(jnp.where(mark, report[:1], 0.0)).astype(jnp.int32))
    wide_ref[...] = jnp.zeros_like(wide_ref)
    for band in range(bands):
        for piece in range(pieces):
            cells = block_ref[band * pieces + piece].astype(jnp.float32)
            for row in range(rows):
                at = (band * rows + row) * chan
                wide_ref[at : at + chan, piece * width : piece * width + cols] = cells[
                    :, row * cols : (row + 1) * cols
                ]
    raw = jnp.dot(
        wide_ref[...].astype(jnp.bfloat16), table_ref[...], preferred_element_type=jnp.float32
    )
    for row in range(lat):
        at = row * chan
        spec_ref[at : at + chan] = (raw[at : at + chan] - means[row] * total_ref[...]) * scales[row]
    for row in range(lat):
        band = numbers[row]
        real = jnp.zeros((chan, bins), jnp.float32)
        imag = jnp.zeros((chan, bins), jnp.float32)
        for tap in range(TAPS):
            source = row + tap - HALO
            if source < 0 or source >= lat:
                continue
            spec_real = spec_ref[source * chan : (source + 1) * chan, :bins]
            spec_imag = spec_ref[source * chan : (source + 1) * chan, bins:]
            kern_real = kern_ref[band * TAPS + tap, :chan]
            kern_imag = kern_ref[band * TAPS + tap, chan:]
            real = real + kern_real * spec_real - kern_imag * spec_imag
            imag = imag + kern_real * spec_imag + kern_imag * spec_real
        prod_ref[row * chan : (row + 1) * chan, :bins] = real
        prod_ref[row * chan : (row + 1) * chan, bins:] = imag
    corr_ref[...] = lax.dot_general(
        (prod_ref[...] * weight_ref[...]).astype(jnp.bfloat16),
        table_ref[...],
        (((1,), (1,)), ((), ())),
        preferred_element_type=jnp.float32,
    )
    for band in range(bands):
        for piece in range(pieces):
            parts = []
            for row in range(rows):
                at = (band * rows + row) * chan
                parts.append(
                    corr_ref[at : at + chan, piece * width : piece * width + cols]
                )
            cells = block_ref[band * pieces + piece].astype(jnp.float32)
            out_ref[band * pieces + piece] = (
                cells + jnp.concatenate(parts, axis=1)
            ).astype(jnp.bfloat16)


def per_device(fields, group_size, band_of_row, basis_spectra, basis_coef, mlp_gain, w_in, w_out):
    row_count, col_count, chan_count = fields.shape
    pieces = lax.axis_size("lon")
    bands = lax.axis_size("lat")
    devices = pieces * bands
    lon_count = col_count * pieces
    lat_count = row_count * bands
    freq_count = lon_count // 2 + 1
    groups = group_size.shape[0]
    pixels = row_count * col_count
    chan = round_up(-(-chan_count // devices), 8)
    active = -(-chan_count // chan)
    width = round_up(col_count, 128)
    bins = round_up(freq_count, 128)
    band_count, _, basis_count = basis_spectra.shape[:3]

    turned = jnp.transpose(fields, (2, 0, 1)).reshape(chan_count, pixels)
    turned = jnp.pad(turned, ((0, active * chan - chan_count), (0, 0)))

    lanes = round_up((2 * groups + 1) * row_count, 128)
    basis = basis_spectra.reshape(band_count * TAPS, basis_count, 2, freq_count)
    arrived, reports, kern = pl.pallas_call(
        functools.partial(
            scatter_body, devices, active, freq_count, row_count, col_count, groups
        ),
        out_shape=[
            jax.ShapeDtypeStruct((devices, chan, pixels), jnp.bfloat16),
            jax.ShapeDtypeStruct((devices, 1, lanes), jnp.float32),
            jax.ShapeDtypeStruct((band_count * TAPS, 2 * chan, bins), jnp.float32),
        ],
        in_specs=[SMEM] * 2 + [VMEM] * 4,
        out_specs=[VMEM] * 3,
        scratch_shapes=[
            pltpu.VMEM((1, lanes), jnp.float32),
        ]
        + [DMA] * 5,
        compiler_params=pltpu.CompilerParams(
            collective_id=0, has_side_effects=True, vmem_limit_bytes=60 * 1024 * 1024
        ),
    )(
        group_size,
        band_of_row,
        turned.reshape(active, chan, pixels),
        turned,
        basis_coef.T,
        basis,
    )
    table, sums, weight = dft_tables(lon_count, pieces, width, bins)
    mixed = pl.pallas_call(
        functools.partial(corr_body, pieces, row_count, col_count, width, bins, groups),
        out_shape=jax.ShapeDtypeStruct((devices, chan, pixels), jnp.bfloat16),
        in_specs=[SMEM] + [VMEM] * 6,
        out_specs=VMEM,
        scratch_shapes=[
            pltpu.VMEM((lat_count * chan, pieces * width), jnp.float32),
            pltpu.VMEM((lat_count * chan, 2 * bins), jnp.float32),
            pltpu.VMEM((lat_count * chan, 2 * bins), jnp.float32),
            pltpu.VMEM((lat_count * chan, pieces * width), jnp.float32),
        ],
        compiler_params=PARAMS,
    )(group_size, arrived, reports, table, sums, weight, kern)
    returned = pl.pallas_call(
        functools.partial(gather_body, devices, active),
        out_shape=jax.ShapeDtypeStruct((active, chan, pixels), jnp.bfloat16),
        in_specs=[VMEM],
        out_specs=VMEM,
        scratch_shapes=[DMA] * 3,
        compiler_params=pltpu.CompilerParams(
            collective_id=1, has_side_effects=True, vmem_limit_bytes=60 * 1024 * 1024
        ),
    )(mixed)
    inputs = returned.reshape(active * chan, pixels)[:chan_count].T.astype(jnp.float32)
    centre = jnp.mean(inputs, axis=-1, keepdims=True)
    spread = jnp.mean((inputs - centre) ** 2, axis=-1, keepdims=True)
    normalised = ((inputs - centre) * lax.rsqrt(spread + EPSILON) * mlp_gain).astype(jnp.bfloat16)
    hidden = jax.nn.gelu(
        jnp.dot(normalised, w_in, preferred_element_type=jnp.float32), approximate=False
    ).astype(jnp.bfloat16)
    result = inputs + jnp.dot(hidden, w_out, preferred_element_type=jnp.float32)
    return result.astype(jnp.bfloat16).reshape(row_count, col_count, chan_count)


def solution(mesh):
    placed = (P("lat", "lon", None), P(), P("lat"), P(), P(), P(), P(), P())
    return jax.shard_map(
        per_device, mesh=mesh, in_specs=placed, out_specs=P("lat", "lon", None), check_vma=False
    )
```
